32 devices in a mesh: tx: 8 (over z, x), ty: 4 (over y, core).
Axes of the slice: x: 2, y: 2, z: 4, core: 2. Of those that a mesh axis runs over, the one named last changes fastest.
Arguments:
- state: float32 [127, 128, 1024], P(None, 'tx', 'ty'), may hold values from -6 to 6
- target: float32 [127, 128, 1024], P(None, 'tx', 'ty'), may hold values from -18 to 18, as said below
- rate: float32 [128, 1024], P('tx', 'ty'), may hold values from 0.05 to 0.15
- face_map: int32 [128, 1024], P('tx', 'ty'), may hold values from 0 to 5
- face_metric: float32 [6], replicated, may hold values from 0.6 to 1.6
- land_mask: int32 [128, 1024], P('tx', 'ty'), may hold values 0 or 1
- w_first: float32 [127, 256], replicated, may hold values from -0.5 to 0.5
- w_second: float32 [256, 256], replicated, may hold values from -0.375 to 0.375
- w_third: float32 [256, 256], replicated, may hold values from -0.375 to 0.375
- w_last: float32 [256, 127], replicated, may hold values from -0.375 to 0.375
Outputs:
- new_state: float32 [127, 128, 1024], P(None, 'tx', 'ty')
- state_grad: float32 [127, 128, 1024], P(None, 'tx', 'ty')
- grad_first: float32 [127, 256], replicated
- grad_second: float32 [256, 256], replicated
- grad_third: float32 [256, 256], replicated
- grad_last: float32 [256, 127], replicated
- loss: float32 [], replicated
The draws below stay inside these ranges and needn't reach their ends.
Inputs may be any that keep to these rules, and one draw needn't show every extreme that they name: `target`: each entry is an ordinary random value times a factor that grows linearly along x from 1 at the first row to 3 at the last.
All inputs are finite; a program needn't handle non-finite values. No bound on the sum of `land_mask` on one device may be relied on, other than what follows from the above.
Results may differ from the reference program's by a relative error of at most 0.0001.
Values sent between devices are 32-bit elements; how exact they have to be, the bound alone decides.
A program may use at most 128 MiB of HBM per device.

```python
import math
import jax
import jax.numpy as jnp
from jax import lax

LEVELS = 127
UNITS = 256
CX = 16
CY = 256
NX = 128
NY = 1024
N_TX = 8
N_TY = 4


def draw_target(key, part):
    ramp = 1.0 + 2.0 * jnp.arange(NX, dtype=jnp.float32) / max(NX - 1, 1)
    base = jnp.clip(jax.random.normal(key, (LEVELS, NX, NY), jnp.float32), -6.0, 6.0)
    return base * ramp[None, :, None]


def plant(values, stream_key, low, largest):
    longest = values.shape.index(max(values.shape))
    spots = []
    for shift in (0, 1):
        where = [jax.random.randint(jax.random.fold_in(stream_key, axis), (), 0, length) for axis, length in enumerate(values.shape)]
        where[longest] = (where[longest] + shift) % values.shape[longest]
        spots.append(tuple(where))
    return values.at[spots[0]].set(low).at[spots[1]].set(largest)


def level_of(own_key, extent, shards, least, high):
    def one(axis_at, shards_of):
        steps = jax.random.uniform(jax.random.fold_in(jax.random.fold_in(own_key, 6), axis_at), (shards_of,), jnp.float32, least / len(shards), high / len(shards))
        return jnp.repeat(jnp.exp(steps), extent[axis_at] // shards_of).reshape((-1,) + (1,) * (len(extent) - axis_at - 1))

    loudness = one(*shards[0])
    for cut in shards[1:]:
        loudness = loudness * one(*cut)
    return loudness


def centred(stream_key, extent, scale, bound, shards=(), held_as=jnp.bfloat16):
    result = jax.random.normal(stream_key, extent, jnp.float32) * scale
    if len(shards) > 0:
        result = level_of(stream_key, extent, shards, -0.22, 0.18) * result
    return jnp.clip(result, min=-bound, max=bound).astype(held_as)


def setup_inputs(seed: int = 0) -> dict:
    key_of = jax.random.split(jax.random.key(seed), 11)
    state = centred(key_of[0], (LEVELS, NX, NY), 1.0, 6.0, ((1, 8), (2, 4)), jnp.float32)
    target = draw_target(jax.random.fold_in(key_of[10], 71), 0)
    rate = jnp.clip(jnp.exp(math.log(0.15) - 1.0986123 * jax.random.uniform(key_of[2], (NX, NY), jnp.float32) ** level_of(key_of[2], (NX, NY), ((0, 8), (1, 4)), -0.2, 0.2)), 0.05, 0.15)
    face_map = plant(jax.random.randint(key_of[3], (NX, NY), 0, 6), jax.random.fold_in(key_of[3], 1), 0, 5).astype(jnp.int32)
    face_metric = jnp.clip(jax.random.uniform(key_of[4], (6,), jnp.float32, 0.6, 1.6), 0.6, 1.6)
    land_mask = plant((jax.random.randint(key_of[5], (NX, NY), 0, 5) < 2).astype(jnp.int32), jax.random.fold_in(key_of[5], 1), 0, 1)
    w_first = centred(key_of[6], (LEVELS, UNITS), LEVELS ** -0.5, 0.5, (), jnp.float32)
    w_second = centred(key_of[7], (UNITS, UNITS), UNITS ** -0.5, 0.375, (), jnp.float32)
    w_third = centred(key_of[8], (UNITS, UNITS), UNITS ** -0.5, 0.375, (), jnp.float32)
    w_last = centred(key_of[9], (UNITS, LEVELS), UNITS ** -0.5, 0.375, (), jnp.float32)
    return {"state": state, "target": target, "rate": rate, "face_map": face_map, "face_metric": face_metric, "land_mask": land_mask, "w_first": w_first, "w_second": w_second, "w_third": w_third, "w_last": w_last}


precise = lax.Precision.HIGHEST

def laplace_roll(grid_field):
    return jnp.roll(grid_field, 1, 1) + jnp.roll(grid_field, -1, 1) + jnp.roll(grid_field, 1, 2) + jnp.roll(grid_field, -1, 2) - 4.0 * grid_field

def face_scale(face_map, face_metric):
    face_ids = jnp.arange(face_metric.shape[0], dtype=jnp.int32)
    picked = (face_map[None, :, :] == face_ids[:, None, None]).astype(jnp.float32)
    return lax.optimization_barrier(jnp.sum(picked * face_metric[:, None, None], axis=0))

def deposit_matrix(levels):
    row_index = lax.broadcasted_iota(jnp.int32, (levels, levels), 0)
    col_index = lax.broadcasted_iota(jnp.int32, (levels, levels), 1)
    return (row_index >= col_index).astype(jnp.float32) / math.sqrt(levels)

def column_pass(columns, targets, land_frac, weights, col_weight):
    w_first, w_second, w_third, w_last = weights
    deposit = deposit_matrix(columns.shape[0])
    first_act = jnp.tanh(jnp.einsum('lh,lc->hc', w_first, columns, precision=precise))
    second_act = jnp.tanh(jnp.einsum('gh,gc->hc', w_second, first_act, precision=precise))
    third_act = jnp.tanh(jnp.einsum('gh,gc->hc', w_third, second_act, precision=precise))
    profile = jnp.einsum('hl,hc->lc', w_last, third_act, precision=precise)
    drag_dep = jnp.dot(deposit, profile, precision=precise)
    updated = columns + land_frac[None, :] * drag_dep
    misfit = updated - targets
    g_flux = jnp.dot(deposit.T, land_frac[None, :] * misfit, precision=precise)
    g_third = jnp.einsum('hl,lc->hc', w_last, g_flux, precision=precise) * (1.0 - third_act * third_act)
    g_second = jnp.einsum('gh,hc->gc', w_third, g_third, precision=precise) * (1.0 - second_act * second_act)
    g_first = jnp.einsum('gh,hc->gc', w_second, g_second, precision=precise) * (1.0 - first_act * first_act)
    adv_grad = misfit + jnp.einsum('lh,hc->lc', w_first, g_first, precision=precise)
    squared = misfit * misfit
    if col_weight is not None:
        columns = columns * col_weight[None, :]
        first_act = first_act * col_weight[None, :]
        second_act = second_act * col_weight[None, :]
        third_act = third_act * col_weight[None, :]
        squared = squared * col_weight[None, :]
    grad_last = jnp.einsum('hc,lc->hl', third_act, g_flux, precision=precise)
    grad_third = jnp.einsum('gc,hc->gh', second_act, g_third, precision=precise)
    grad_second = jnp.einsum('gc,hc->gh', first_act, g_second, precision=precise)
    grad_first = jnp.einsum('lc,hc->lh', columns, g_first, precision=precise)
    return (updated, adv_grad, (grad_first, grad_second, grad_third, grad_last), jnp.sum(squared))

def reference(state, target, rate, face_map, face_metric, land_mask, w_first, w_second, w_third, w_last):
    levels = state.shape[0]
    diffusion = rate * face_scale(face_map, face_metric)
    advanced = state + diffusion[None] * laplace_roll(state)
    block_count = N_TX * N_TY
    block_cols = CX * CY

    def to_blocks(grid_field):
        return grid_field.reshape(levels, block_count, block_cols).transpose(1, 0, 2)
    land_blocks = land_mask.astype(jnp.float32).reshape(block_count, block_cols)
    weights = (w_first, w_second, w_third, w_last)

    def scan_block(running, block_items):
        totals, squares = running
        updated, adv_grad, gradients, part_sq = column_pass(block_items[0], block_items[1], block_items[2], weights, None)
        totals = tuple((left + right for left, right in zip(totals, gradients)))
        return ((totals, squares + part_sq), (updated, adv_grad))
    empty_grads = tuple((jnp.zeros(weight.shape, jnp.float32) for weight in weights))
    (totals, squares), (new_blocks, grad_blocks) = lax.scan(scan_block, (empty_grads, jnp.zeros((), jnp.float32)), (to_blocks(advanced), to_blocks(target), land_blocks))
    new_state = new_blocks.transpose(1, 0, 2).reshape(levels, NX, NY)
    adv_grad = grad_blocks.transpose(1, 0, 2).reshape(levels, NX, NY)
    state_grad = adv_grad + laplace_roll(diffusion[None] * adv_grad)
    columns_all = NX * NY
    grad_scale = 1.0 / math.sqrt(columns_all)
    loss = 0.5 * squares / columns_all
    return (new_state, state_grad, totals[0] * grad_scale, totals[1] * grad_scale, totals[2] * grad_scale, totals[3] * grad_scale, loss)
```

```python
import functools
import math

import jax
import jax.numpy as jnp
from jax import lax
from jax.experimental import pallas as pl
from jax.experimental.pallas import tpu as pltpu
from jax.sharding import PartitionSpec as P

MESH = pl.DeviceIdType.MESH
precise = lax.Precision.HIGHEST


def log2(n):
    return n.bit_length() - 1


def groups_of(n_tx, n_ty):
    sizes = {"tx": n_tx, "ty": n_ty}
    first = [b for b in (("ty", 0), ("tx", 0), ("ty", 1)) if b[1] < log2(sizes[b[0]])]
    rest = [(axis, b) for axis in ("tx", "ty") for b in range(log2(sizes[axis])) if (axis, b) not in first]
    return [first] + [rest[k : k + 3] for k in range(0, len(rest), 3)]


def bit_of(me, dim):
    return (me[dim[0]] // (1 << dim[1])) % 2


def partner(me, group, mask):
    at = dict(me)
    for j, dim in enumerate(group):
        if mask >> j & 1:
            at[dim[0]] = at[dim[0]] + (1 - 2 * bit_of(me, dim)) * (1 << dim[1])
    return (at["tx"], at["ty"])


def place(me, group, mask):
    total = 0
    for j, dim in enumerate(group):
        bit = bit_of(me, dim)
        total = total + (1 - bit if mask >> j & 1 else bit) * (1 << j)
    return total


class Sum:
    def __init__(self, groups, me, src, acc, recv, out, sems, s, finish):
        self.groups, self.me, self.s, self.finish = groups, me, s, finish
        self.src, self.acc, self.recv, self.out, self.sems = src, acc, recv, out, sems
        self.offset, self.length, self.base = 0, src.shape[0], 0
        self.step, self.copies, self.walked = 0, [], []

    def send(self):
        n = len(self.groups)
        t = self.step
        scatter = t < n
        group = self.groups[t] if scatter else self.groups[2 * n - 1 - t]
        count = 1 << len(group)
        if scatter:
            self.walked.append((self.offset, self.length))
            self.length //= count
        self.copies = []
        for mask in range(1, count):
            if scatter:
                give = pl.multiple_of(self.offset + place(self.me, group, mask) * self.length, 8)
                src = (self.src if t == 0 else self.acc).at[pl.ds(give, self.length)]
                dst = self.recv.at[pl.ds(self.base + (mask - 1) * self.length, self.length)]
            else:
                src = dst = self.out.at[pl.ds(self.offset, self.length)]
            copy = pltpu.make_async_remote_copy(
                src_ref=src,
                dst_ref=dst,
                send_sem=self.sems.at[0, self.s, t, mask],
                recv_sem=self.sems.at[1, self.s, t, mask],
                device_id=partner(self.me, group, mask),
                device_id_type=MESH,
            )
            copy.start()
            self.copies.append(copy)
        if scatter:
            self.offset = pl.multiple_of(self.offset + place(self.me, group, 0) * self.length, 8)

    def receive(self):
        n = len(self.groups)
        t = self.step
        for copy in self.copies:
            copy.wait()
        if t < n:
            rows = pl.ds(self.offset, self.length)
            src = self.src if t == 0 else self.acc
            dst = self.out if t == n - 1 else self.acc
            total = src[rows, :]
            for k in range(len(self.copies)):
                total = total + self.recv[pl.ds(self.base + k * self.length, self.length), :]
            dst[rows, :] = total
            self.base += len(self.copies) * self.length
        else:
            self.offset, self.length = self.walked[2 * n - 1 - t]
        self.step += 1

    @property
    def done(self):
        return self.step == 2 * len(self.groups)


def split(x):
    high = x.astype(jnp.bfloat16)
    return high, (x - high.astype(jnp.float32)).astype(jnp.bfloat16)


def weights3(w):
    high, low = split(w)
    return jnp.concatenate([high, low, high], axis=1)


def times(w3, high, low):
    return jnp.dot(w3, jnp.concatenate([high, high, low], axis=0), preferred_element_type=jnp.float32)


def outer(h, g):
    hh, hl = h
    gh, gl = g
    return lax.dot_general(
        jnp.concatenate([hh, hl, hh], axis=1),
        jnp.concatenate([gh, gh, gl], axis=1),
        (((1,), (1,)), ((), ())),
        preferred_element_type=jnp.float32,
    )


def window_kernel(
    n_tx, n_ty, chunk,
    state, target, rate, face_map, face_metric, land_mask, w1, w2, w3, w4,
    new_state, state_grad, o1, o2, o3, o4, loss,
    sum1, sum2, sum3, sum4, w1p,
    x, a, m, u, tg, cf, lf, h1, h2, h3, ga, gb,
    w1t, w2t, w3t, wdt, w1n, w2n, w3n, wdn, sq,
    s1, s2, s3, s4, a1, a2, a3, a4, r1, r2, r3, r4,
    hx, hy, py, sems, halo_sems,
):
    levels, tile_rows, cols = state.shape
    units = w2.shape[0]
    width = tile_rows * cols
    deep = x.shape[0]
    f32 = jnp.float32
    me = {"tx": lax.axis_index("tx"), "ty": lax.axis_index("ty")}
    up = (lax.rem(me["tx"] + n_tx - 1, n_tx), me["ty"])
    down = (lax.rem(me["tx"] + 1, n_tx), me["ty"])
    left = (me["tx"], lax.rem(me["ty"] + n_ty - 1, n_ty))
    right = (me["tx"], lax.rem(me["ty"] + 1, n_ty))
    groups = groups_of(n_tx, n_ty)

    barrier = pltpu.get_barrier_semaphore()
    others = [partner(me, g, mask) for g in groups for mask in range(1, 1 << len(g))] + [up, down, left, right]
    for other in others:
        pl.semaphore_signal(barrier, inc=1, device_id=other, device_id_type=MESH)

    def row(i):
        return pl.ds(i * cols, cols)

    for buf in (x, m, tg):
        buf[deep - 8 :, :] = jnp.zeros((8, width), f32)
    for i in range(tile_rows):
        x[0:levels, row(i)] = state[:, i, :]
    lane = lax.broadcasted_iota(jnp.int32, (deep, 128), 1)
    wide = lax.broadcasted_iota(jnp.int32, (deep, cols), 1)

    def pack(field, start, shift):
        packed = jnp.zeros((deep, 128), f32)
        for i in range(tile_rows):
            block = field[:, pl.ds(i * cols + start, 128)]
            turn = (i + shift) % 128
            packed = jnp.where(lane == i, pltpu.roll(block, turn, 1) if turn else block, packed)
        return packed

    def exchange(e, field):
        py[e, 0] = pack(field, cols - 128, 1)
        py[e, 1] = pack(field, 0, 0)
        moves = (
            (field.at[:, row(tile_rows - 1)], hx.at[e, 0], down),
            (field.at[:, row(0)], hx.at[e, 1], up),
            (py.at[e, 0], hy.at[e, 0], right),
            (py.at[e, 1], hy.at[e, 1], left),
        )
        copies = []
        for k, (src, dst, to) in enumerate(moves):
            copy = pltpu.make_async_remote_copy(
                src_ref=src,
                dst_ref=dst,
                send_sem=halo_sems.at[0, e, k],
                recv_sem=halo_sems.at[1, e, k],
                device_id=to,
                device_id_type=MESH,
            )
            copy.start()
            copies.append(copy)
        return copies

    def laplace(e, field, i):
        here = field[:, row(i)]
        above = hx[e, 0] if i == 0 else field[:, row(i - 1)]
        below = hx[e, 1] if i == tile_rows - 1 else field[:, row(i + 1)]
        west = jnp.where(wide == 0, hy[e, 0][:, i : i + 1], pltpu.roll(here, 1, 1))
        east = jnp.where(wide == cols - 1, hy[e, 1][:, i : i + 1], pltpu.roll(here, cols - 1, 1))
        return above + below + west + east - 4.0 * here

    pl.semaphore_wait(barrier, len(others))
    copies = exchange(0, x)

    scale = jnp.zeros(rate.shape, f32)
    faces = face_map[...]
    for k in range(face_metric.shape[0]):
        scale = jnp.where(faces == k, face_metric[k], scale)
    coeff = rate[...] * scale
    land = land_mask[...].astype(f32)
    for i in range(tile_rows):
        cf[:, row(i)] = coeff[i : i + 1, :]
        lf[:, row(i)] = land[i : i + 1, :]
        tg[0:levels, row(i)] = target[:, i, :]
    l_index = lax.broadcasted_iota(jnp.int32, (levels, deep), 0)
    m_index = lax.broadcasted_iota(jnp.int32, (levels, deep), 1)
    deposit = jnp.where((l_index <= m_index) & (m_index < levels), 1.0 / math.sqrt(levels), 0.0)
    wd = jnp.dot(w4[...], deposit, precision=precise, preferred_element_type=f32)
    wdn[...] = weights3(wd)
    wdt[...] = weights3(wd.T)
    w1p[deep - 8 :, :] = jnp.zeros((8, units), f32)
    w1p[0:levels, :] = w1[...]
    w1n[...] = weights3(w1p[...])
    w1t[...] = weights3(w1p[...].T)
    w2n[...] = weights3(w2[...])
    w2t[...] = weights3(w2[...].T)
    w3n[...] = weights3(w3[...])
    w3t[...] = weights3(w3[...].T)

    for copy in copies:
        copy.wait()
    for i in range(tile_rows):
        a[:, row(i)] = x[:, row(i)] + cf[:, row(i)] * laplace(0, x, i)

    count = width // chunk
    sq[...] = jnp.zeros_like(sq)

    def loop(low, high, step):
        def once(k, carry):
            step(pl.ds(pl.multiple_of(k * chunk, chunk), chunk))
            return carry

        lax.fori_loop(low, high, once, 0)

    def forward(at):
        start = a[:, at]
        h = jnp.tanh(times(w1t[...], *split(start)))
        h1[:, at] = h
        h = jnp.tanh(times(w2t[...], *split(h)))
        h2[:, at] = h
        h = jnp.tanh(times(w3t[...], *split(h)))
        h3[:, at] = h
        drag = times(wdt[...], *split(h))
        updated = start + lf[:, at] * drag
        u[:, at] = updated
        misfit = updated - tg[:, at]
        m[:, at] = misfit
        sq[...] += jnp.sum(misfit * misfit, axis=0, keepdims=True)

    def add_to(total, value):
        for half in range(units // 128):
            rows = pl.ds(half * value.shape[0], value.shape[0])
            total[rows, :] += value[:, half * 128 : (half + 1) * 128]

    def back_last(at):
        g = split(lf[:, at] * m[:, at])
        h = h3[:, at]
        add_to(s4, outer(g, split(h)))
        ga[:, at] = times(wdn[...], *g) * (1.0 - h * h)

    def back_third(at):
        g = split(ga[:, at])
        h = h2[:, at]
        add_to(s3, outer(split(h), g))
        gb[:, at] = times(w3n[...], *g) * (1.0 - h * h)

    def back_second(at):
        g = split(gb[:, at])
        h = h1[:, at]
        add_to(s2, outer(split(h), g))
        ga[:, at] = times(w2n[...], *g) * (1.0 - h * h)

    def back_first(at):
        add_to(s1, outer(split(a[:, at]), split(ga[:, at])))

    def adjoint(at):
        adv = m[:, at] + times(w1n[...], *split(ga[:, at]))
        m[:, at] = adv
        x[:, at] = cf[:, at] * adv

    for total in (s1, s2, s3, s4):
        total[...] = jnp.zeros_like(total)
    loop(0, count, forward)
    live = []

    def begin(src, acc, recv, out, s, finish):
        live.append(Sum(groups, me, src, acc, recv, out, sems, s, finish))
        live[-1].send()

    def advance():
        for item in live:
            if not item.done:
                item.receive()
                if not item.done:
                    item.send()
                else:
                    item.finish()

    factor = 1.0 / math.sqrt(width * n_tx * n_ty)

    def whole(total, rows):
        return jnp.concatenate([total[k * rows : (k + 1) * rows, :] for k in range(units // 128)], axis=1)

    def finish_last():
        up_index = lax.broadcasted_iota(jnp.int32, (deep, levels), 0)
        to_index = lax.broadcasted_iota(jnp.int32, (deep, levels), 1)
        lower = jnp.where((to_index <= up_index) & (up_index < levels), 1.0 / math.sqrt(levels), 0.0)
        raw = whole(sum4, deep).T
        o4[...] = jnp.dot(raw, lower, precision=precise, preferred_element_type=f32) * factor

    def finish_third():
        o3[...] = whole(sum3, units) * factor

    def finish_second():
        o2[...] = whole(sum2, units) * factor

    def finish_first():
        full = whole(sum1, deep)
        o1[...] = full[0:levels] * factor
        loss[0, 0] = jnp.sum(full[levels : levels + 1]) * (0.5 / (width * n_tx * n_ty))

    loop(0, count, back_last)
    begin(s4, a4, r4, sum4, 3, finish_last)
    loop(0, count, back_third)
    advance()
    begin(s3, a3, r3, sum3, 2, finish_third)
    loop(0, count, back_second)
    advance()
    begin(s2, a2, r2, sum2, 1, finish_second)
    loop(0, count, back_first)
    advance()
    for part in range(units // 128):
        squares = jnp.zeros((1, 128), f32)
        if part == 0:
            for k in range(chunk // 128):
                squares = squares + sq[:, k * 128 : (k + 1) * 128]
        s1[part * deep + levels : part * deep + levels + 1, :] = squares
    begin(s1, a1, r1, sum1, 0, finish_first)
    loop(0, count, adjoint)
    copies = exchange(1, x)
    advance()
    for i in range(tile_rows):
        new_state[:, i, :] = u[0:levels, row(i)]
    advance()
    for copy in copies:
        copy.wait()
    for i in range(tile_rows):
        state_grad[:, i, :] = (m[:, row(i)] + laplace(1, x, i))[0:levels]
        if i == tile_rows // 2 - 1:
            advance()
    while not all(item.done for item in live):
        advance()


def deliver(*refs):
    *refs, sems = refs
    half = len(refs) // 2
    copies = [pltpu.make_async_copy(refs[k], refs[half + k], sems.at[k]) for k in range(half)]
    for copy in copies:
        copy.start()
    for copy in copies:
        copy.wait()


def body(n_tx, n_ty, state, target, rate, face_map, face_metric, land_mask, w_first, w_second, w_third, w_last):
    levels, tile_rows, tile_cols = state.shape
    units = w_second.shape[0]
    width = tile_rows * tile_cols
    deep = -(-(levels + 1) // 8) * 8
    chunk = min(1024, width)
    unit = 8 * n_tx * n_ty
    f32, bf16 = jnp.float32, jnp.bfloat16

    def padded(rows):
        return -(-rows // unit) * unit

    lanes = units // 128
    small, large = padded(lanes * deep), padded(lanes * units)
    sizes = (small, large, large, small)
    steps = 2 * len(groups_of(n_tx, n_ty))
    vmem = pl.BlockSpec(memory_space=pltpu.VMEM)
    scratch = (
        [pltpu.VMEM((r, 128), f32) for r in sizes]
        + [pltpu.VMEM((deep, units), f32)]
        + [pltpu.VMEM((deep, width), f32)] * 5
        + [pltpu.VMEM((1, width), f32)] * 2
        + [pltpu.VMEM((units, width), f32)] * 5
        + [
            pltpu.VMEM((units, 3 * deep), bf16),
            pltpu.VMEM((units, 3 * units), bf16),
            pltpu.VMEM((units, 3 * units), bf16),
            pltpu.VMEM((deep, 3 * units), bf16),
            pltpu.VMEM((deep, 3 * units), bf16),
            pltpu.VMEM((units, 3 * units), bf16),
            pltpu.VMEM((units, 3 * units), bf16),
            pltpu.VMEM((units, 3 * deep), bf16),
            pltpu.VMEM((1, chunk), f32),
        ]
        + [pltpu.VMEM((r, 128), f32) for r in sizes] * 3
        + [
            pltpu.VMEM((2, 2, deep, tile_cols), f32),
            pltpu.VMEM((2, 2, deep, 128), f32),
            pltpu.VMEM((2, 2, deep, 128), f32),
            pltpu.SemaphoreType.DMA((2, 4, steps, 8)),
            pltpu.SemaphoreType.DMA((2, 2, 4)),
        ]
    )
    outs = (state, state, w_first, w_second, w_third, w_last)
    *results, loss = pl.pallas_call(
        functools.partial(window_kernel, n_tx, n_ty, chunk),
        out_shape=[pltpu.VMEM(o.shape, f32) for o in outs] + [jax.ShapeDtypeStruct((1, 1), f32)],
        in_specs=[vmem] * 4 + [pl.BlockSpec(memory_space=pltpu.SMEM)] + [vmem] * 5,
        out_specs=[vmem] * 6 + [pl.BlockSpec(memory_space=pltpu.SMEM)],
        scratch_shapes=scratch,
        compiler_params=pltpu.CompilerParams(
            collective_id=0, has_side_effects=True, vmem_limit_bytes=57 * 2**20
        ),
        name="window",
    )(state, target, rate, face_map, face_metric, land_mask, w_first, w_second, w_third, w_last)
    results = pl.pallas_call(
        deliver,
        out_shape=[jax.ShapeDtypeStruct(o.shape, f32) for o in outs],
        in_specs=[pl.BlockSpec(memory_space=pl.ANY)] * len(outs),
        out_specs=[pl.BlockSpec(memory_space=pl.ANY)] * len(outs),
        scratch_shapes=[pltpu.SemaphoreType.DMA((len(outs),))],
        compiler_params=pltpu.CompilerParams(vmem_limit_bytes=2**20),
        name="deliver",
    )(*results)
    return (*results, loss.reshape(()))


def solution(mesh):
    tile, flat, copied = P(None, "tx", "ty"), P("tx", "ty"), P()
    return jax.shard_map(
        functools.partial(body, mesh.shape["tx"], mesh.shape["ty"]),
        mesh=mesh,
        in_specs=(tile, tile, flat, flat, copied, flat, copied, copied, copied, copied),
        out_specs=(tile, tile, copied, copied, copied, copied, copied),
        check_vma=False,
    )
```

```python
import functools
import math

import jax
import jax.numpy as jnp
from jax import lax
from jax.experimental import pallas as pl
from jax.experimental.pallas import tpu as pltpu
from jax.sharding import PartitionSpec as P

MESH = pl.DeviceIdType.MESH
precise = lax.Precision.HIGHEST


def log2(n):
    return n.bit_length() - 1


def plans_of(n_tx, n_ty):
    rest = [("ty", b) for b in range(1, log2(n_ty))] + [("tx", b) for b in range(log2(n_tx))]
    wide = [[("ty", 0)]] * (n_ty > 1) + [rest[k : k + 4] for k in range(0, len(rest), 4)]
    return [wide] * 4


def bit_of(me, dim):
    return (me[dim[0]] // (1 << dim[1])) % 2


def partner(me, group, mask):
    at = dict(me)
    for j, dim in enumerate(group):
        if mask >> j & 1:
            at[dim[0]] = at[dim[0]] + (1 - 2 * bit_of(me, dim)) * (1 << dim[1])
    return (at["tx"], at["ty"])


def place(me, group, mask):
    total = 0
    for j, dim in enumerate(group):
        bit = bit_of(me, dim)
        total = total + (1 - bit if mask >> j & 1 else bit) * (1 << j)
    return total


class Sum:
    def __init__(self, groups, me, src, acc, recv, out, sems, s, finish):
        self.groups, self.me, self.s, self.finish = groups, me, s, finish
        self.src, self.acc, self.recv, self.out, self.sems = src, acc, recv, out, sems
        self.offset, self.length, self.base = 0, src.shape[0], 0
        self.step, self.copies, self.walked = 0, [], []

    def send(self):
        n = len(self.groups)
        t = self.step
        scatter = t < n
        group = self.groups[t] if scatter else self.groups[2 * n - 1 - t]
        count = 1 << len(group)
        if scatter:
            self.walked.append((self.offset, self.length))
            self.length //= count
        self.copies = []
        for mask in range(1, count):
            if scatter:
                give = pl.multiple_of(self.offset + place(self.me, group, mask) * self.length, 8)
                src = (self.src if t == 0 else self.acc).at[pl.ds(give, self.length)]
                dst = self.recv.at[pl.ds(self.base + (mask - 1) * self.length, self.length)]
            else:
                src = dst = self.out.at[pl.ds(self.offset, self.length)]
            copy = pltpu.make_async_remote_copy(
                src_ref=src,
                dst_ref=dst,
                send_sem=self.sems.at[0, self.s, t, mask],
                recv_sem=self.sems.at[1, self.s, t, mask],
                device_id=partner(self.me, group, mask),
                device_id_type=MESH,
            )
            copy.start()
            self.copies.append(copy)
        if scatter:
            self.offset = pl.multiple_of(self.offset + place(self.me, group, 0) * self.length, 8)

    def receive(self):
        n = len(self.groups)
        t = self.step
        for copy in self.copies:
            copy.wait()
        if t < n:
            rows = pl.ds(self.offset, self.length)
            src = self.src if t == 0 else self.acc
            dst = self.out if t == n - 1 else self.acc
            total = src[rows, :]
            for k in range(len(self.copies)):
                total = total + self.recv[pl.ds(self.base + k * self.length, self.length), :]
            dst[rows, :] = total
            self.base += len(self.copies) * self.length
        else:
            self.offset, self.length = self.walked[2 * n - 1 - t]
        self.step += 1

    @property
    def done(self):
        return self.step == 2 * len(self.groups)


def split(x):
    high = x.astype(jnp.bfloat16)
    return high, (x - high.astype(jnp.float32)).astype(jnp.bfloat16)


def weights3(w):
    high, low = split(w)
    return jnp.concatenate([high, low, high], axis=1)


def times(w3, high, low):
    return jnp.dot(w3, jnp.concatenate([high, high, low], axis=0), preferred_element_type=jnp.float32)


def nt(p, q):
    return lax.dot_general(p, q, (((1,), (1,)), ((), ())), preferred_element_type=jnp.float32)


def outer(h, g):
    hh, hl = h
    gh, gl = g
    return nt(jnp.concatenate([hh, hl, hh], axis=1), jnp.concatenate([gh, gh, gl], axis=1))


def outer_thin(p, q):
    ph, pl_ = p
    qh, ql = q
    rows = ph.shape[0]
    both = nt(jnp.concatenate([ph, pl_], axis=0), qh)
    return both[:rows] + both[rows:] + nt(ph, ql)


def window_kernel(
    n_tx, n_ty, chunk,
    state_in, target_in, rate, face_map, face_metric, land_mask, w1_in, w2_in, w3_in, w4_in,
    new_state, state_grad, o1, o2, o3, o4, loss,
    sum1, sum2, sum3, sum4, w1p,
    state, target, w1, w2, w3, w4,
    x, a, m, tg, cf, lf, h1, h2, h3, ga, gb,
    w1t, w2t, w3t, wdt, w1n, w2n, w3n, wdn, sq,
    s1, s2, s3, s4, a1, a2, a3, a4, r1, r2, r3, r4,
    hx, hy, py, in_sems, sems, halo_sems,
):
    levels, tile_rows, cols = state.shape
    units = w2.shape[0]
    width = tile_rows * cols
    deep = x.shape[0]
    f32 = jnp.float32
    me = {"tx": lax.axis_index("tx"), "ty": lax.axis_index("ty")}
    up = (lax.rem(me["tx"] + n_tx - 1, n_tx), me["ty"])
    down = (lax.rem(me["tx"] + 1, n_tx), me["ty"])
    left = (me["tx"], lax.rem(me["ty"] + n_ty - 1, n_ty))
    right = (me["tx"], lax.rem(me["ty"] + 1, n_ty))
    plans = plans_of(n_tx, n_ty)

    barrier = pltpu.get_barrier_semaphore()
    flips = sorted(
        {tuple(d for j, d in enumerate(g) if k >> j & 1) for plan in plans for g in plan for k in range(1, 1 << len(g))}
    )
    others = [partner(me, dims, (1 << len(dims)) - 1) for dims in flips] + [up, down, left, right]
    for other in others:
        pl.semaphore_signal(barrier, inc=1, device_id=other, device_id_type=MESH)

    loads = []
    for k, (src, dst) in enumerate(
        ((state_in, state), (w4_in, w4), (w1_in, w1), (w2_in, w2), (w3_in, w3), (target_in, target))
    ):
        loads.append(pltpu.make_async_copy(src, dst, in_sems.at[k]))
        loads[-1].start()

    def row(i):
        return pl.ds(i * cols, cols)

    for buf in (x, m, tg):
        buf[deep - 8 :, :] = jnp.zeros((8, width), f32)
    w1p[deep - 8 :, :] = jnp.zeros((8, units), f32)
    sq[...] = jnp.zeros_like(sq)
    for total in (s1, s2, s3, s4):
        total[...] = jnp.zeros_like(total)
    lane = lax.broadcasted_iota(jnp.int32, (deep, 128), 1)
    wide = lax.broadcasted_iota(jnp.int32, (deep, cols), 1)

    def pack(field, start, shift):
        packed = jnp.zeros((deep, 128), f32)
        for i in range(tile_rows):
            block = field[:, pl.ds(i * cols + start, 128)]
            turn = (i + shift) % 128
            packed = jnp.where(lane == i, pltpu.roll(block, turn, 1) if turn else block, packed)
        return packed

    def exchange(e, first, moves):
        copies = []
        for k, (src, dst, to) in enumerate(moves):
            copy = pltpu.make_async_remote_copy(
                src_ref=src,
                dst_ref=dst,
                send_sem=halo_sems.at[0, e, first + k],
                recv_sem=halo_sems.at[1, e, first + k],
                device_id=to,
                device_id_type=MESH,
            )
            copy.start()
            copies.append(copy)
        return copies

    def exchange_rows(e, field):
        return exchange(
            e, 0, ((field.at[:, row(tile_rows - 1)], hx.at[e, 0], down), (field.at[:, row(0)], hx.at[e, 1], up))
        )

    def exchange_columns(e, field):
        py[e, 0] = pack(field, cols - 128, 1)
        py[e, 1] = pack(field, 0, 0)
        return exchange(e, 2, ((py.at[e, 0], hy.at[e, 0], right), (py.at[e, 1], hy.at[e, 1], left)))

    def laplace(e, field, i):
        here = field[:, row(i)]
        above = hx[e, 0] if i == 0 else field[:, row(i - 1)]
        below = hx[e, 1] if i == tile_rows - 1 else field[:, row(i + 1)]
        west = jnp.where(wide == 0, hy[e, 0][:, i : i + 1], pltpu.roll(here, 1, 1))
        east = jnp.where(wide == cols - 1, hy[e, 1][:, i : i + 1], pltpu.roll(here, cols - 1, 1))
        return above + below + west + east - 4.0 * here

    loads[0].wait()
    for i in (0, tile_rows - 1):
        x[0:levels, row(i)] = state[:, i, :]
    pl.semaphore_wait(barrier, len(others))
    row_copies = exchange_rows(0, x)
    for i in range(1, tile_rows - 1):
        x[0:levels, row(i)] = state[:, i, :]
    column_copies = exchange_columns(0, x)

    scale = jnp.zeros(rate.shape, f32)
    faces = face_map[...]
    for k in range(face_metric.shape[0]):
        scale = jnp.where(faces == k, face_metric[k], scale)
    coeff = rate[...] * scale
    land = land_mask[...].astype(f32)
    for i in range(tile_rows):
        cf[:, row(i)] = coeff[i : i + 1, :]
        lf[:, row(i)] = land[i : i + 1, :]
    l_index = lax.broadcasted_iota(jnp.int32, (levels, deep), 0)
    m_index = lax.broadcasted_iota(jnp.int32, (levels, deep), 1)
    deposit = jnp.where((l_index <= m_index) & (m_index < levels), 1.0 / math.sqrt(levels), 0.0)
    loads[1].wait()
    wd = jnp.dot(w4[...], deposit, precision=precise, preferred_element_type=f32)
    wdn[...] = weights3(wd)
    wdt[...] = weights3(wd.T)
    loads[2].wait()
    w1p[0:levels, :] = w1[...]
    w1n[...] = weights3(w1p[...])
    w1t[...] = weights3(w1p[...].T)
    loads[3].wait()
    w2n[...] = weights3(w2[...])
    w2t[...] = weights3(w2[...].T)
    loads[4].wait()
    w3n[...] = weights3(w3[...])
    w3t[...] = weights3(w3[...].T)
    loads[5].wait()

    count = width // chunk
    deal = chunk // cols
    edges = [0, count - 1] if count > 1 else [0]
    middle = list(range(1, count - 1))

    def columns(c):
        return pl.ds(c * chunk, chunk)

    def rows_of(c):
        return range(c * deal, (c + 1) * deal)

    def forward(group):
        for c in group:
            for i in rows_of(c):
                a[:, row(i)] = x[:, row(i)] + cf[:, row(i)] * laplace(0, x, i)
                tg[0:levels, row(i)] = target[:, i, :]
        for w, src, dst in ((w1t, a, h1), (w2t, h1, h2), (w3t, h2, h3)):
            for c in group:
                dst[:, columns(c)] = jnp.tanh(times(w[...], *split(src[:, columns(c)])))
        for c in group:
            at = columns(c)
            updated = a[:, at] + lf[:, at] * times(wdt[...], *split(h3[:, at]))
            misfit = updated - tg[:, at]
            m[:, at] = misfit
            sq[...] += jnp.sum(misfit * misfit, axis=0, keepdims=True)
            for k, i in enumerate(rows_of(c)):
                new_state[:, i, :] = updated[0:levels, k * cols : (k + 1) * cols]

    def add_to(total, value):
        for half in range(units // 128):
            rows = pl.ds(half * value.shape[0], value.shape[0])
            total[rows, :] += value[:, half * 128 : (half + 1) * 128]

    def back_last(c):
        at = columns(c)
        g = split(lf[:, at] * m[:, at])
        h = h3[:, at]
        add_to(s4, outer_thin(g, split(h)))
        ga[:, at] = times(wdn[...], *g) * (1.0 - h * h)

    def back_third(c):
        at = columns(c)
        g = split(ga[:, at])
        h = h2[:, at]
        add_to(s3, outer(split(h), g))
        gb[:, at] = times(w3n[...], *g) * (1.0 - h * h)

    def back_second(c):
        at = columns(c)
        g = split(gb[:, at])
        h = h1[:, at]
        add_to(s2, outer(split(h), g))
        ga[:, at] = times(w2n[...], *g) * (1.0 - h * h)

    def back_first(c):
        at = columns(c)
        add_to(s1, outer_thin(split(a[:, at]), split(ga[:, at])))

    def adjoint(c):
        at = columns(c)
        adv = m[:, at] + times(w1n[...], *split(ga[:, at]))
        m[:, at] = adv
        x[:, at] = cf[:, at] * adv

    live = []

    def begin(src, acc, recv, out, s, finish):
        live.append(Sum(plans[s], me, src, acc, recv, out, sems, s, finish))
        live[-1].send()

    def advance(*which):
        for k in which:
            item = live[k]
            if not item.done:
                item.receive()
                if not item.done:
                    item.send()
                else:
                    item.finish()

    factor = 1.0 / math.sqrt(width * n_tx * n_ty)

    def whole(total, rows):
        return jnp.concatenate([total[k * rows : (k + 1) * rows, :] for k in range(units // 128)], axis=1)

    def finish_last():
        up_index = lax.broadcasted_iota(jnp.int32, (deep, levels), 0)
        to_index = lax.broadcasted_iota(jnp.int32, (deep, levels), 1)
        lower = jnp.where((to_index <= up_index) & (up_index < levels), 1.0 / math.sqrt(levels), 0.0)
        raw = whole(sum4, deep).T
        o4[...] = jnp.dot(raw, lower, precision=precise, preferred_element_type=f32) * factor

    def finish_third():
        o3[...] = whole(sum3, units) * factor

    def finish_second():
        o2[...] = whole(sum2, units) * factor

    def finish_first():
        full = whole(sum1, deep)
        o1[...] = full[0:levels] * factor
        loss[0, 0] = jnp.sum(full[levels : levels + 1]) * (0.5 / (width * n_tx * n_ty))

    for copy in column_copies:
        copy.wait()
    if middle:
        forward(middle)
    for copy in row_copies:
        copy.wait()
    forward(edges)

    for c in edges + middle:
        back_last(c)
    begin(s4, a4, r4, sum4, 3, finish_last)
    for c in edges:
        back_third(c)
    advance(0)
    for c in middle:
        back_third(c)
    begin(s3, a3, r3, sum3, 2, finish_third)
    for c in edges:
        back_second(c)
    advance(1)
    for c in edges:
        adjoint(c)
    row_copies = exchange_rows(1, x)
    for c in middle:
        back_second(c)
    begin(s2, a2, r2, sum2, 1, finish_second)
    advance(0)
    for c in range(count):
        back_first(c)
    for part in range(units // 128):
        squares = jnp.zeros((1, 128), f32)
        if part == 0:
            for k in range(chunk // 128):
                squares = squares + sq[:, k * 128 : (k + 1) * 128]
        s1[part * deep + levels : part * deep + levels + 1, :] = squares
    begin(s1, a1, r1, sum1, 0, finish_first)
    advance(2)
    for c in middle:
        adjoint(c)
    advance(3)
    column_copies = exchange_columns(1, x)
    advance(1, 0)

    def finish_rows(rows):
        for i in rows:
            state_grad[:, i, :] = (m[:, row(i)] + laplace(1, x, i))[0:levels]

    for copy in column_copies:
        copy.wait()
    finish_rows(range(1, tile_rows - 1))
    advance(2, 3)
    for copy in row_copies:
        copy.wait()
    finish_rows((0, tile_rows - 1))
    while not all(item.done for item in live):
        advance(*range(len(live)))


def deliver(*refs):
    *refs, sems = refs
    half = len(refs) // 2
    copies = [pltpu.make_async_copy(refs[k], refs[half + k], sems.at[k]) for k in range(half)]
    for copy in copies:
        copy.start()
    for copy in copies:
        copy.wait()


def body(n_tx, n_ty, state, target, rate, face_map, face_metric, land_mask, w_first, w_second, w_third, w_last):
    levels, tile_rows, tile_cols = state.shape
    units = w_second.shape[0]
    width = tile_rows * tile_cols
    deep = -(-(levels + 1) // 8) * 8
    chunk = min(1024, width)
    unit = 8 * n_tx * n_ty
    f32, bf16 = jnp.float32, jnp.bfloat16

    def padded(rows):
        return -(-rows // unit) * unit

    lanes = units // 128
    small, large = padded(lanes * deep), padded(lanes * units)
    sizes = (small, large, large, small)
    steps = 2 * max(len(plan) for plan in plans_of(n_tx, n_ty))
    anywhere = pl.BlockSpec(memory_space=pl.ANY)
    vmem = pl.BlockSpec(memory_space=pltpu.VMEM)
    scratch = (
        [pltpu.VMEM((r, 128), f32) for r in sizes]
        + [pltpu.VMEM((deep, units), f32)]
        + [pltpu.VMEM(w.shape, f32) for w in (state, target, w_first, w_second, w_third, w_last)]
        + [pltpu.VMEM((deep, width), f32)] * 4
        + [pltpu.VMEM((1, width), f32)] * 2
        + [pltpu.VMEM((units, width), f32)] * 5
        + [
            pltpu.VMEM((units, 3 * deep), bf16),
            pltpu.VMEM((units, 3 * units), bf16),
            pltpu.VMEM((units, 3 * units), bf16),
            pltpu.VMEM((deep, 3 * units), bf16),
            pltpu.VMEM((deep, 3 * units), bf16),
            pltpu.VMEM((units, 3 * units), bf16),
            pltpu.VMEM((units, 3 * units), bf16),
            pltpu.VMEM((units, 3 * deep), bf16),
            pltpu.VMEM((1, chunk), f32),
        ]
        + [pltpu.VMEM((r, 128), f32) for r in sizes] * 3
        + [
            pltpu.VMEM((2, 2, deep, tile_cols), f32),
            pltpu.VMEM((2, 2, deep, 128), f32),
            pltpu.VMEM((2, 2, deep, 128), f32),
            pltpu.SemaphoreType.DMA((6,)),
            pltpu.SemaphoreType.DMA((2, 4, steps, 16)),
            pltpu.SemaphoreType.DMA((2, 2, 4)),
        ]
    )
    outs = (state, state, w_first, w_second, w_third, w_last)
    *results, loss = pl.pallas_call(
        functools.partial(window_kernel, n_tx, n_ty, chunk),
        out_shape=[pltpu.VMEM(o.shape, f32) for o in outs] + [jax.ShapeDtypeStruct((1, 1), f32)],
        in_specs=[anywhere] * 2 + [vmem] * 2 + [pl.BlockSpec(memory_space=pltpu.SMEM), vmem] + [anywhere] * 4,
        out_specs=[vmem] * 6 + [pl.BlockSpec(memory_space=pltpu.SMEM)],
        scratch_shapes=scratch,
        compiler_params=pltpu.CompilerParams(
            collective_id=0, has_side_effects=True, vmem_limit_bytes=57 * 2**20
        ),
        name="window",
    )(state, target, rate, face_map, face_metric, land_mask, w_first, w_second, w_third, w_last)
    results = pl.pallas_call(
        deliver,
        out_shape=[jax.ShapeDtypeStruct(o.shape, f32) for o in outs],
        in_specs=[pl.BlockSpec(memory_space=pl.ANY)] * len(outs),
        out_specs=[pl.BlockSpec(memory_space=pl.ANY)] * len(outs),
        scratch_shapes=[pltpu.SemaphoreType.DMA((len(outs),))],
        compiler_params=pltpu.CompilerParams(vmem_limit_bytes=2**20),
        name="deliver",
    )(*results)
    return (*results, loss.reshape(()))


def solution(mesh):
    tile, flat, copied = P(None, "tx", "ty"), P("tx", "ty"), P()
    return jax.shard_map(
        functools.partial(body, mesh.shape["tx"], mesh.shape["ty"]),
        mesh=mesh,
        in_specs=(tile, tile, flat, flat, copied, flat, copied, copied, copied, copied),
        out_specs=(tile, tile, copied, copied, copied, copied, copied),
        check_vma=False,
    )
```

```python
import functools
import math

import jax
import jax.numpy as jnp
from jax import lax
from jax.experimental import pallas as pl
from jax.experimental.pallas import tpu as pltpu
from jax.sharding import PartitionSpec as P

MESH = pl.DeviceIdType.MESH
precise = lax.Precision.HIGHEST


def log2(n):
    return n.bit_length() - 1


def plan_of(n_tx, n_ty):
    rest = [("ty", b) for b in range(2, log2(n_ty))] + [("tx", b) for b in range(1, log2(n_tx))]
    near = [[("ty", 0)]] * (n_ty > 1) + [[("ty", 1)] * (n_ty > 2) + [("tx", 0)] * (n_tx > 1)]
    far, last = rest[:-2], rest[-2:]
    return [g for g in near + [far[k : k + 3] for k in range(0, len(far), 3)] if g], last


def landing(plan, rows):
    scatters, last = plan
    total = 0
    for group in scatters:
        rows //= 1 << len(group)
        total += rows * ((1 << len(group)) - 1)
    return total + rows * (1 << len(last))


def bit_of(me, dim):
    return (me[dim[0]] // (1 << dim[1])) % 2


def partner(me, group, mask):
    at = dict(me)
    for j, dim in enumerate(group):
        if mask >> j & 1:
            at[dim[0]] = at[dim[0]] + (1 - 2 * bit_of(me, dim)) * (1 << dim[1])
    return (at["tx"], at["ty"])


def place(me, group, mask):
    total = 0
    for j, dim in enumerate(group):
        bit = bit_of(me, dim)
        total = total + (1 - bit if mask >> j & 1 else bit) * (1 << j)
    return total


class Sum:
    def __init__(self, plan, me, src, acc, recv, out, sems, s, finish):
        self.scatters, self.last = plan
        self.me, self.s, self.finish = me, s, finish
        self.src, self.acc, self.recv, self.out, self.sems = src, acc, recv, out, sems
        self.offset, self.length, self.base = 0, src.shape[0], 0
        self.step, self.copies, self.sent, self.walked = 0, [], [], []

    def send(self):
        n, t = len(self.scatters), self.step
        group = self.scatters[t] if t < n else self.last if t == n else self.scatters[2 * n - t]
        count = 1 << len(group)
        held = self.src if t == 0 else self.acc
        if t < n:
            self.walked.append((self.offset, self.length))
            self.length //= count
        elif t == n:
            mine = pl.multiple_of(self.base + place(self.me, group, 0) * self.length, 8)
            slot = self.recv.at[pl.ds(mine, self.length)]
            slot[...] = held[pl.ds(self.offset, self.length), :]
        self.copies = []
        for mask in range(1, count):
            if t < n:
                give = pl.multiple_of(self.offset + place(self.me, group, mask) * self.length, 8)
                src = held.at[pl.ds(give, self.length)]
                dst = self.recv.at[pl.ds(self.base + (mask - 1) * self.length, self.length)]
            elif t == n:
                src, dst = held.at[pl.ds(self.offset, self.length)], slot
            else:
                src = dst = self.out.at[pl.ds(self.offset, self.length)]
            copy = pltpu.make_async_remote_copy(
                src_ref=src,
                dst_ref=dst,
                send_sem=self.sems.at[0, self.s, t, mask],
                recv_sem=self.sems.at[1, self.s, t, mask],
                device_id=partner(self.me, group, mask),
                device_id_type=MESH,
            )
            copy.start()
            self.copies.append(copy)
        if t < n:
            self.offset = pl.multiple_of(self.offset + place(self.me, group, 0) * self.length, 8)

    def receive(self):
        n, t = len(self.scatters), self.step
        for copy in self.copies:
            copy.wait_recv()
        self.sent += self.copies

        def landed(k):
            return self.recv[pl.ds(self.base + k * self.length, self.length), :]

        rows = pl.ds(self.offset, self.length)
        if t < n:
            total = (self.src if t == 0 else self.acc)[rows, :]
            for k in range(len(self.copies)):
                total = total + landed(k)
            self.acc[rows, :] = total
            self.base += len(self.copies) * self.length
        elif t == n:
            total = landed(0)
            for k in range(1, 1 << len(self.last)):
                total = total + landed(k)
            self.out[rows, :] = total
        else:
            self.offset, self.length = self.walked[2 * n - t]
        self.step += 1

    def drain(self):
        for copy in self.sent:
            copy.wait_send()

    @property
    def done(self):
        return self.step == 2 * len(self.scatters) + 1


def split(x):
    high = x.astype(jnp.bfloat16)
    return high, (x - high.astype(jnp.float32)).astype(jnp.bfloat16)


def weights3(w):
    high, low = split(w)
    return jnp.concatenate([high, low, high], axis=1)


def times(w3, high, low):
    return jnp.dot(w3, jnp.concatenate([high, high, low], axis=0), preferred_element_type=jnp.float32)


def nt(p, q):
    return lax.dot_general(p, q, (((1,), (1,)), ((), ())), preferred_element_type=jnp.float32)


def outer(h, g):
    hh, hl = h
    gh, gl = g
    return nt(jnp.concatenate([hh, hl, hh], axis=1), jnp.concatenate([gh, gh, gl], axis=1))


def outer_thin(p, q):
    ph, pl_ = p
    qh, ql = q
    rows = ph.shape[0]
    both = nt(jnp.concatenate([ph, pl_], axis=0), qh)
    return both[:rows] + both[rows:] + nt(ph, ql)


def window_kernel(
    n_tx, n_ty, chunk,
    state_in, target_in, rate, face_map, face_metric, land_mask, w1_in, w2_in, w3_in, w4_in,
    new_state, state_grad, o1, o2, o3, o4, loss,
    sum1, sum2, sum3, sum4, w1p,
    state, target, w1, w2, w3, w4,
    x, a, m, tg, cf, lf, h1, h2, h3, ga, gb,
    w1t, w2t, w3t, wdt, w1n, w2n, w3n, wdn, sq,
    s1, s2, s3, s4, a1, a2, a3, a4, r1, r2, r3, r4,
    hx, hy, py, rim, in_sems, sems, halo_sems,
):
    levels, tile_rows, cols = state.shape
    units = w2.shape[0]
    width = tile_rows * cols
    deep = x.shape[0]
    f32 = jnp.float32
    me = {"tx": lax.axis_index("tx"), "ty": lax.axis_index("ty")}
    up = (lax.rem(me["tx"] + n_tx - 1, n_tx), me["ty"])
    down = (lax.rem(me["tx"] + 1, n_tx), me["ty"])
    left = (me["tx"], lax.rem(me["ty"] + n_ty - 1, n_ty))
    right = (me["tx"], lax.rem(me["ty"] + 1, n_ty))
    plan = plan_of(n_tx, n_ty)

    barrier = pltpu.get_barrier_semaphore()
    flips = sorted(
        {tuple(d for j, d in enumerate(g) if k >> j & 1) for g in plan[0] + [plan[1]] for k in range(1, 1 << len(g))}
    )
    others = [partner(me, dims, (1 << len(dims)) - 1) for dims in flips] + [up, down, left, right]
    for other in others:
        pl.semaphore_signal(barrier, inc=1, device_id=other, device_id_type=MESH)

    loads = []
    for k, (src, dst) in enumerate(
        ((state_in, state), (w4_in, w4), (w1_in, w1), (w2_in, w2), (w3_in, w3), (target_in, target))
    ):
        loads.append(pltpu.make_async_copy(src, dst, in_sems.at[k]))

    loads[0].start()

    def row(i):
        return pl.ds(i * cols, cols)

    for buf in (x, m, tg):
        buf[deep - 8 :, :] = jnp.zeros((8, width), f32)
    w1p[deep - 8 :, :] = jnp.zeros((8, units), f32)
    sq[...] = jnp.zeros_like(sq)
    for total in (s1, s2, s3, s4):
        total[...] = jnp.zeros_like(total)
    lane = lax.broadcasted_iota(jnp.int32, (deep, 128), 1)
    wide = lax.broadcasted_iota(jnp.int32, (deep, cols), 1)

    def pack(field, start, shift):
        packed = jnp.zeros((deep, 128), f32)
        for i in range(tile_rows):
            block = field[:, pl.ds(i * cols + start, 128)]
            turn = (i + shift) % 128
            packed = jnp.where(lane == i, pltpu.roll(block, turn, 1) if turn else block, packed)
        return packed

    def exchange(e, first, moves):
        copies = []
        for k, (src, dst, to) in enumerate(moves):
            copy = pltpu.make_async_remote_copy(
                src_ref=src,
                dst_ref=dst,
                send_sem=halo_sems.at[0, e, first + k],
                recv_sem=halo_sems.at[1, e, first + k],
                device_id=to,
                device_id_type=MESH,
            )
            copy.start()
            copies.append(copy)
        return copies

    def exchange_rows(e, field):
        return exchange(
            e, 0, ((field.at[:, row(tile_rows - 1)], hx.at[e, 0], down), (field.at[:, row(0)], hx.at[e, 1], up))
        )

    def exchange_columns(e, field):
        py[e, 0] = pack(field, cols - 128, 1).T[0:tile_rows]
        py[e, 1] = pack(field, 0, 0).T[0:tile_rows]
        return exchange(e, 2, ((py.at[e, 0], hy.at[e, 0], right), (py.at[e, 1], hy.at[e, 1], left)))

    def turn_columns(e):
        for side in range(2):
            rim[side] = hy[e, side].T

    def laplace(e, field, i):
        here = field[:, row(i)]
        above = hx[e, 0] if i == 0 else field[:, row(i - 1)]
        below = hx[e, 1] if i == tile_rows - 1 else field[:, row(i + 1)]
        west = jnp.where(wide == 0, rim[0][:, i : i + 1], pltpu.roll(here, 1, 1))
        east = jnp.where(wide == cols - 1, rim[1][:, i : i + 1], pltpu.roll(here, cols - 1, 1))
        return above + below + west + east - 4.0 * here

    loads[0].wait()
    for load in loads[1:]:
        load.start()
    for i in (0, tile_rows - 1):
        x[0:levels, row(i)] = state[:, i, :]
    pl.semaphore_wait(barrier, len(others))
    row_copies = exchange_rows(0, x)
    for i in range(1, tile_rows - 1):
        x[0:levels, row(i)] = state[:, i, :]
    column_copies = exchange_columns(0, x)

    scale = jnp.zeros(rate.shape, f32)
    faces = face_map[...]
    for k in range(face_metric.shape[0]):
        scale = jnp.where(faces == k, face_metric[k], scale)
    coeff = rate[...] * scale
    land = land_mask[...].astype(f32)
    for i in range(tile_rows):
        cf[:, row(i)] = coeff[i : i + 1, :]
        lf[:, row(i)] = land[i : i + 1, :]
    l_index = lax.broadcasted_iota(jnp.int32, (levels, deep), 0)
    m_index = lax.broadcasted_iota(jnp.int32, (levels, deep), 1)
    deposit = jnp.where((l_index <= m_index) & (m_index < levels), 1.0 / math.sqrt(levels), 0.0)
    loads[1].wait()
    wd = jnp.dot(w4[...], deposit, precision=precise, preferred_element_type=f32)
    wdn[...] = weights3(wd)
    wdt[...] = weights3(wd.T)
    loads[2].wait()
    w1p[0:levels, :] = w1[...]
    w1n[...] = weights3(w1p[...])
    w1t[...] = weights3(w1p[...].T)
    loads[3].wait()
    w2n[...] = weights3(w2[...])
    w2t[...] = weights3(w2[...].T)
    loads[4].wait()
    w3n[...] = weights3(w3[...])
    w3t[...] = weights3(w3[...].T)
    loads[5].wait()

    count = width // chunk
    deal = chunk // cols
    edges = [0, count - 1] if count > 1 else [0]
    middle = list(range(1, count - 1))

    def columns(c):
        return pl.ds(c * chunk, chunk)

    def rows_of(c):
        return range(c * deal, (c + 1) * deal)

    def forward(group):
        for c in group:
            for i in rows_of(c):
                a[:, row(i)] = x[:, row(i)] + cf[:, row(i)] * laplace(0, x, i)
                tg[0:levels, row(i)] = target[:, i, :]
        for w, src, dst in ((w1t, a, h1), (w2t, h1, h2), (w3t, h2, h3)):
            for c in group:
                dst[:, columns(c)] = jnp.tanh(times(w[...], *split(src[:, columns(c)])))
        for c in group:
            at = columns(c)
            updated = a[:, at] + lf[:, at] * times(wdt[...], *split(h3[:, at]))
            misfit = updated - tg[:, at]
            m[:, at] = misfit
            sq[...] += jnp.sum(misfit * misfit, axis=0, keepdims=True)
            for k, i in enumerate(rows_of(c)):
                new_state[:, i, :] = updated[0:levels, k * cols : (k + 1) * cols]

    def add_to(total, value):
        for half in range(units // 128):
            rows = pl.ds(half * value.shape[0], value.shape[0])
            total[rows, :] += value[:, half * 128 : (half + 1) * 128]

    def back_last(c):
        at = columns(c)
        g = split(lf[:, at] * m[:, at])
        h = h3[:, at]
        add_to(s4, outer_thin(g, split(h)))
        ga[:, at] = times(wdn[...], *g) * (1.0 - h * h)

    def back_third(c):
        at = columns(c)
        g = split(ga[:, at])
        h = h2[:, at]
        add_to(s3, outer(split(h), g))
        gb[:, at] = times(w3n[...], *g) * (1.0 - h * h)

    def back_second(c):
        at = columns(c)
        g = split(gb[:, at])
        h = h1[:, at]
        add_to(s2, outer(split(h), g))
        ga[:, at] = times(w2n[...], *g) * (1.0 - h * h)

    def back_first(c):
        at = columns(c)
        add_to(s1, outer_thin(split(a[:, at]), split(ga[:, at])))

    def adjoint(c):
        at = columns(c)
        adv = m[:, at] + times(w1n[...], *split(ga[:, at]))
        m[:, at] = adv
        x[:, at] = cf[:, at] * adv

    live = []

    def begin(src, acc, recv, out, s, finish):
        live.append(Sum(plan, me, src, acc, recv, out, sems, s, finish))
        live[-1].send()

    def advance(*which):
        for k in which:
            item = live[k]
            if not item.done:
                item.receive()
                if not item.done:
                    item.send()
                else:
                    item.finish()

    factor = 1.0 / math.sqrt(width * n_tx * n_ty)

    def whole(total, rows):
        return jnp.concatenate([total[k * rows : (k + 1) * rows, :] for k in range(units // 128)], axis=1)

    def finish_last():
        up_index = lax.broadcasted_iota(jnp.int32, (deep, levels), 0)
        to_index = lax.broadcasted_iota(jnp.int32, (deep, levels), 1)
        lower = jnp.where((to_index <= up_index) & (up_index < levels), 1.0 / math.sqrt(levels), 0.0)
        raw = whole(sum4, deep).T
        o4[...] = jnp.dot(raw, lower, precision=precise, preferred_element_type=f32) * factor

    def finish_third():
        o3[...] = whole(sum3, units) * factor

    def finish_second():
        o2[...] = whole(sum2, units) * factor

    def finish_first():
        full = whole(sum1, deep)
        o1[...] = full[0:levels] * factor
        loss[0, 0] = jnp.sum(full[levels : levels + 1]) * (0.5 / (width * n_tx * n_ty))

    for copy in column_copies:
        copy.wait()
    turn_columns(0)
    if middle:
        forward(middle)
    for copy in row_copies:
        copy.wait()
    forward(edges)

    for c in edges + middle:
        back_last(c)
    begin(s4, a4, r4, sum4, 3, finish_last)
    for c in edges:
        back_third(c)
    advance(0)
    for c in middle:
        back_third(c)
    begin(s3, a3, r3, sum3, 2, finish_third)
    for c in edges:
        back_second(c)
    for c in edges:
        adjoint(c)
    row_copies = exchange_rows(1, x)
    advance(1, 0)
    for c in middle:
        back_second(c)
    begin(s2, a2, r2, sum2, 1, finish_second)
    for c in range(count):
        back_first(c)
    for part in range(units // 128):
        squares = jnp.zeros((1, 128), f32)
        if part == 0:
            for k in range(chunk // 128):
                squares = squares + sq[:, k * 128 : (k + 1) * 128]
        s1[part * deep + levels : part * deep + levels + 1, :] = squares
    begin(s1, a1, r1, sum1, 0, finish_first)
    advance(2, 1)
    for c in middle:
        adjoint(c)
    column_copies = exchange_columns(1, x)
    advance(3, 0)

    def finish_rows(rows):
        for i in rows:
            state_grad[:, i, :] = (m[:, row(i)] + laplace(1, x, i))[0:levels]

    for copy in column_copies:
        copy.wait()
    turn_columns(1)
    advance(2, 1)
    finish_rows(range(1, tile_rows - 1))
    advance(3, 0)
    for copy in row_copies:
        copy.wait()
    finish_rows((0, tile_rows - 1))
    while not all(item.done for item in live):
        advance(2, 3, 1, 0)
    for item in live:
        item.drain()


def deliver(*refs):
    *refs, sems = refs
    half = len(refs) // 2
    copies = [pltpu.make_async_copy(refs[k], refs[half + k], sems.at[k]) for k in range(half)]
    for copy in copies:
        copy.start()
    for copy in copies:
        copy.wait()


def body(n_tx, n_ty, state, target, rate, face_map, face_metric, land_mask, w_first, w_second, w_third, w_last):
    levels, tile_rows, tile_cols = state.shape
    units = w_second.shape[0]
    width = tile_rows * tile_cols
    deep = -(-(levels + 1) // 8) * 8
    chunk = min(1024, width)
    unit = 8 * n_tx * n_ty
    f32, bf16 = jnp.float32, jnp.bfloat16

    def padded(rows):
        return -(-rows // unit) * unit

    lanes = units // 128
    small, large = padded(lanes * deep), padded(lanes * units)
    sizes = (small, large, large, small)
    plan = plan_of(n_tx, n_ty)
    steps = 2 * len(plan[0]) + 1
    anywhere = pl.BlockSpec(memory_space=pl.ANY)
    vmem = pl.BlockSpec(memory_space=pltpu.VMEM)
    scratch = (
        [pltpu.VMEM((r, 128), f32) for r in sizes]
        + [pltpu.VMEM((deep, units), f32)]
        + [pltpu.VMEM(w.shape, f32) for w in (state, target, w_first, w_second, w_third, w_last)]
        + [pltpu.VMEM((deep, width), f32)] * 4
        + [pltpu.VMEM((1, width), f32)] * 2
        + [pltpu.VMEM((units, width), f32)] * 5
        + [
            pltpu.VMEM((units, 3 * deep), bf16),
            pltpu.VMEM((units, 3 * units), bf16),
            pltpu.VMEM((units, 3 * units), bf16),
            pltpu.VMEM((deep, 3 * units), bf16),
            pltpu.VMEM((deep, 3 * units), bf16),
            pltpu.VMEM((units, 3 * units), bf16),
            pltpu.VMEM((units, 3 * units), bf16),
            pltpu.VMEM((units, 3 * deep), bf16),
            pltpu.VMEM((1, chunk), f32),
        ]
        + [pltpu.VMEM((r, 128), f32) for r in sizes] * 2
        + [pltpu.VMEM((landing(plan, r), 128), f32) for r in sizes]
        + [
            pltpu.VMEM((2, 2, deep, tile_cols), f32),
            pltpu.VMEM((2, 2, tile_rows, deep), f32),
            pltpu.VMEM((2, 2, tile_rows, deep), f32),
            pltpu.VMEM((2, deep, tile_rows), f32),
            pltpu.SemaphoreType.DMA((6,)),
            pltpu.SemaphoreType.DMA((2, 4, steps, 8)),
            pltpu.SemaphoreType.DMA((2, 2, 4)),
        ]
    )
    outs = (state, state, w_first, w_second, w_third, w_last)
    *results, loss = pl.pallas_call(
        functools.partial(window_kernel, n_tx, n_ty, chunk),
        out_shape=[pltpu.VMEM(o.shape, f32) for o in outs] + [jax.ShapeDtypeStruct((1, 1), f32)],
        in_specs=[anywhere] * 2 + [vmem] * 2 + [pl.BlockSpec(memory_space=pltpu.SMEM), vmem] + [anywhere] * 4,
        out_specs=[vmem] * 6 + [pl.BlockSpec(memory_space=pltpu.SMEM)],
        scratch_shapes=scratch,
        compiler_params=pltpu.CompilerParams(
            collective_id=0, has_side_effects=True, vmem_limit_bytes=57 * 2**20
        ),
        name="window",
    )(state, target, rate, face_map, face_metric, land_mask, w_first, w_second, w_third, w_last)
    results = pl.pallas_call(
        deliver,
        out_shape=[jax.ShapeDtypeStruct(o.shape, f32) for o in outs],
        in_specs=[pl.BlockSpec(memory_space=pl.ANY)] * len(outs),
        out_specs=[pl.BlockSpec(memory_space=pl.ANY)] * len(outs),
        scratch_shapes=[pltpu.SemaphoreType.DMA((len(outs),))],
        compiler_params=pltpu.CompilerParams(vmem_limit_bytes=2**20),
        name="deliver",
    )(*results)
    return (*results, loss.reshape(()))


def solution(mesh):
    tile, flat, copied = P(None, "tx", "ty"), P("tx", "ty"), P()
    return jax.shard_map(
        functools.partial(body, mesh.shape["tx"], mesh.shape["ty"]),
        mesh=mesh,
        in_specs=(tile, tile, flat, flat, copied, flat, copied, copied, copied, copied),
        out_specs=(tile, tile, copied, copied, copied, copied, copied),
        check_vma=False,
    )
```

```python
import functools
import math

import jax
import jax.numpy as jnp
from jax import lax
from jax.experimental import pallas as pl
from jax.experimental.pallas import tpu as pltpu
from jax.sharding import PartitionSpec as P

MESH = pl.DeviceIdType.MESH
precise = lax.Precision.HIGHEST


def log2(n):
    return n.bit_length() - 1


def plan_of(n_tx, n_ty):
    rest = [("ty", b) for b in range(2, log2(n_ty))] + [("tx", b) for b in range(1, log2(n_tx))]
    near = [[("ty", 0)]] * (n_ty > 1) + [[("ty", 1)] * (n_ty > 2) + [("tx", 0)] * (n_tx > 1)]
    far, last = rest[:-2], rest[-2:]
    return [g for g in near + [far[k : k + 3] for k in range(0, len(far), 3)] if g], last


def landing(plan, rows):
    scatters, last = plan
    total = 0
    for group in scatters:
        rows //= 1 << len(group)
        total += rows * ((1 << len(group)) - 1)
    return total + rows * (1 << len(last))


def bit_of(me, dim):
    return (me[dim[0]] // (1 << dim[1])) % 2


def partner(me, group, mask):
    at = dict(me)
    for j, dim in enumerate(group):
        if mask >> j & 1:
            at[dim[0]] = at[dim[0]] + (1 - 2 * bit_of(me, dim)) * (1 << dim[1])
    return (at["tx"], at["ty"])


def place(me, group, mask):
    total = 0
    for j, dim in enumerate(group):
        bit = bit_of(me, dim)
        total = total + (1 - bit if mask >> j & 1 else bit) * (1 << j)
    return total


class Sum:
    def __init__(self, plan, me, src, acc, recv, out, sems, s, finish):
        self.scatters, self.last = plan
        self.me, self.s, self.finish = me, s, finish
        self.src, self.acc, self.recv, self.out, self.sems = src, acc, recv, out, sems
        self.offset, self.length, self.base = 0, src.shape[0], 0
        self.step, self.copies, self.sent, self.walked = 0, [], [], []

    def send(self):
        n, t = len(self.scatters), self.step
        group = self.scatters[t] if t < n else self.last if t == n else self.scatters[2 * n - t]
        count = 1 << len(group)
        held = self.src if t == 0 else self.acc
        if t < n:
            self.walked.append((self.offset, self.length))
            self.length //= count
        elif t == n:
            mine = pl.multiple_of(self.base + place(self.me, group, 0) * self.length, 8)
            slot = self.recv.at[pl.ds(mine, self.length)]
            slot[...] = held[pl.ds(self.offset, self.length), :]
        self.copies = []
        for mask in range(1, count):
            if t < n:
                give = pl.multiple_of(self.offset + place(self.me, group, mask) * self.length, 8)
                src = held.at[pl.ds(give, self.length)]
                dst = self.recv.at[pl.ds(self.base + (mask - 1) * self.length, self.length)]
            elif t == n:
                src, dst = held.at[pl.ds(self.offset, self.length)], slot
            else:
                src = dst = self.out.at[pl.ds(self.offset, self.length)]
            copy = pltpu.make_async_remote_copy(
                src_ref=src,
                dst_ref=dst,
                send_sem=self.sems.at[0, self.s, t, mask],
                recv_sem=self.sems.at[1, self.s, t, mask],
                device_id=partner(self.me, group, mask),
                device_id_type=MESH,
            )
            copy.start()
            self.copies.append(copy)
        if t < n:
            self.offset = pl.multiple_of(self.offset + place(self.me, group, 0) * self.length, 8)

    def receive(self):
        n, t = len(self.scatters), self.step
        for copy in self.copies:
            copy.wait_recv()
        self.sent += self.copies

        def landed(k):
            return self.recv[pl.ds(self.base + k * self.length, self.length), :]

        rows = pl.ds(self.offset, self.length)
        if t < n:
            total = (self.src if t == 0 else self.acc)[rows, :]
            for k in range(len(self.copies)):
                total = total + landed(k)
            self.acc[rows, :] = total
            self.base += len(self.copies) * self.length
        elif t == n:
            total = landed(0)
            for k in range(1, 1 << len(self.last)):
                total = total + landed(k)
            self.out[rows, :] = total
        else:
            self.offset, self.length = self.walked[2 * n - t]
        self.step += 1

    def drain(self):
        for copy in self.sent:
            copy.wait_send()

    @property
    def done(self):
        return self.step == 2 * len(self.scatters) + 1


def split(x):
    high = x.astype(jnp.bfloat16)
    return high, (x - high.astype(jnp.float32)).astype(jnp.bfloat16)


def weights3(w):
    high, low = split(w)
    return jnp.concatenate([high, low, high], axis=1)


def times(w3, high, low):
    return jnp.dot(w3, jnp.concatenate([high, high, low], axis=0), preferred_element_type=jnp.float32)


def nt(p, q):
    return lax.dot_general(p, q, (((1,), (1,)), ((), ())), preferred_element_type=jnp.float32)


def outer(h, g):
    hh, hl = h
    gh, gl = g
    return nt(jnp.concatenate([hh, hl, hh], axis=1), jnp.concatenate([gh, gh, gl], axis=1))


def outer_thin(p, q):
    ph, pl_ = p
    qh, ql = q
    rows = ph.shape[0]
    both = nt(jnp.concatenate([ph, pl_], axis=0), qh)
    return both[:rows] + both[rows:] + nt(ph, ql)


def window_kernel(
    n_tx, n_ty, chunk,
    state_in, target_in, rate, face_map, face_metric, land_mask, w1_in, w2_in, w3_in, w4_in,
    new_state, state_grad, o1, o2, o3, o4, loss,
    sum1, sum2, sum3, sum4, w1p,
    state, target, w1, w2, w3, w4,
    x, a, m, tg, cf, lf, h1, h2, h3, ga, gb,
    w1t, w2t, w3t, wdt, w1n, w2n, w3n, wdn, sq,
    s1, s2, s3, s4, a1, a2, a3, a4, r1, r2, r3, r4,
    hx, hy, py, rim, in_sems, sems, halo_sems,
):
    levels, tile_rows, cols = state.shape
    units = w2.shape[0]
    width = tile_rows * cols
    deep = x.shape[0]
    f32 = jnp.float32
    me = {"tx": lax.axis_index("tx"), "ty": lax.axis_index("ty")}
    up = (lax.rem(me["tx"] + n_tx - 1, n_tx), me["ty"])
    down = (lax.rem(me["tx"] + 1, n_tx), me["ty"])
    left = (me["tx"], lax.rem(me["ty"] + n_ty - 1, n_ty))
    right = (me["tx"], lax.rem(me["ty"] + 1, n_ty))
    plan = plan_of(n_tx, n_ty)

    barrier = pltpu.get_barrier_semaphore()
    flips = sorted(
        {tuple(d for j, d in enumerate(g) if k >> j & 1) for g in plan[0] + [plan[1]] for k in range(1, 1 << len(g))}
    )
    others = [partner(me, dims, (1 << len(dims)) - 1) for dims in flips] + [up, down, left, right]
    for other in others:
        pl.semaphore_signal(barrier, inc=1, device_id=other, device_id_type=MESH)

    loads = []
    for k, (src, dst) in enumerate(
        ((state_in, state), (w4_in, w4), (w1_in, w1), (w2_in, w2), (w3_in, w3), (target_in, target))
    ):
        loads.append(pltpu.make_async_copy(src, dst, in_sems.at[k]))

    loads[0].start()

    def row(i):
        return pl.ds(i * cols, cols)

    for buf in (x, m, tg):
        buf[deep - 8 :, :] = jnp.zeros((8, width), f32)
    w1p[deep - 8 :, :] = jnp.zeros((8, units), f32)
    sq[...] = jnp.zeros_like(sq)
    for total in (s1, s2, s3, s4):
        total[...] = jnp.zeros_like(total)
    lane = lax.broadcasted_iota(jnp.int32, (deep, 128), 1)
    wide = lax.broadcasted_iota(jnp.int32, (deep, cols), 1)

    def pack(field, start, shift):
        packed = jnp.zeros((deep, 128), f32)
        for i in range(tile_rows):
            block = field[:, pl.ds(i * cols + start, 128)]
            turn = (i + shift) % 128
            packed = jnp.where(lane == i, pltpu.roll(block, turn, 1) if turn else block, packed)
        return packed

    def exchange(e, first, moves):
        copies = []
        for k, (src, dst, to) in enumerate(moves):
            copy = pltpu.make_async_remote_copy(
                src_ref=src,
                dst_ref=dst,
                send_sem=halo_sems.at[0, e, first + k],
                recv_sem=halo_sems.at[1, e, first + k],
                device_id=to,
                device_id_type=MESH,
            )
            copy.start()
            copies.append(copy)
        return copies

    def exchange_rows(e, field):
        return exchange(
            e, 0, ((field.at[:, row(tile_rows - 1)], hx.at[e, 0], down), (field.at[:, row(0)], hx.at[e, 1], up))
        )

    def exchange_columns(e, field):
        py[e, 0] = pack(field, cols - 128, 1).T[0:tile_rows]
        py[e, 1] = pack(field, 0, 0).T[0:tile_rows]
        return exchange(e, 2, ((py.at[e, 0], hy.at[e, 0], right), (py.at[e, 1], hy.at[e, 1], left)))

    def turn_columns(e):
        for side in range(2):
            rim[side] = hy[e, side].T

    def laplace(e, field, i):
        here = field[:, row(i)]
        above = hx[e, 0] if i == 0 else field[:, row(i - 1)]
        below = hx[e, 1] if i == tile_rows - 1 else field[:, row(i + 1)]
        west = jnp.where(wide == 0, rim[0][:, i : i + 1], pltpu.roll(here, 1, 1))
        east = jnp.where(wide == cols - 1, rim[1][:, i : i + 1], pltpu.roll(here, cols - 1, 1))
        return above + below + west + east - 4.0 * here

    loads[0].wait()
    for load in loads[1:]:
        load.start()
    for i in (0, tile_rows - 1):
        x[0:levels, row(i)] = state[:, i, :]
    pl.semaphore_wait(barrier, len(others))
    row_copies = exchange_rows(0, x)
    for i in range(1, tile_rows - 1):
        x[0:levels, row(i)] = state[:, i, :]
    column_copies = exchange_columns(0, x)

    scale = jnp.zeros(rate.shape, f32)
    faces = face_map[...]
    for k in range(face_metric.shape[0]):
        scale = jnp.where(faces == k, face_metric[k], scale)
    coeff = rate[...] * scale
    land = land_mask[...].astype(f32)
    for i in range(tile_rows):
        cf[:, row(i)] = coeff[i : i + 1, :]
        lf[:, row(i)] = land[i : i + 1, :]
    l_index = lax.broadcasted_iota(jnp.int32, (levels, deep), 0)
    m_index = lax.broadcasted_iota(jnp.int32, (levels, deep), 1)
    deposit = jnp.where((l_index <= m_index) & (m_index < levels), 1.0 / math.sqrt(levels), 0.0)
    loads[1].wait()
    wd = jnp.dot(w4[...], deposit, precision=precise, preferred_element_type=f32)
    wdn[...] = weights3(wd)
    wdt[...] = weights3(wd.T)
    loads[2].wait()
    w1p[0:levels, :] = w1[...]
    w1n[...] = weights3(w1p[...])
    w1t[...] = weights3(w1p[...].T)
    loads[3].wait()
    w2n[...] = weights3(w2[...])
    w2t[...] = weights3(w2[...].T)
    loads[4].wait()
    w3n[...] = weights3(w3[...])
    w3t[...] = weights3(w3[...].T)
    loads[5].wait()

    count = width // chunk
    deal = chunk // cols
    edges = [0, count - 1] if count > 1 else [0]
    middle = list(range(1, count - 1))

    def columns(c):
        return pl.ds(c * chunk, chunk)

    def rows_of(c):
        return range(c * deal, (c + 1) * deal)

    def forward(group):
        for c in group:
            for i in rows_of(c):
                a[:, row(i)] = x[:, row(i)] + cf[:, row(i)] * laplace(0, x, i)
            h1[:, columns(c)] = jnp.tanh(times(w1t[...], *split(a[:, columns(c)])))
        for c in group:
            for i in rows_of(c):
                tg[0:levels, row(i)] = target[:, i, :]
        for w, src, dst in ((w2t, h1, h2), (w3t, h2, h3)):
            for c in group:
                dst[:, columns(c)] = jnp.tanh(times(w[...], *split(src[:, columns(c)])))
        for c in group:
            at = columns(c)
            updated = a[:, at] + lf[:, at] * times(wdt[...], *split(h3[:, at]))
            misfit = updated - tg[:, at]
            m[:, at] = misfit
            sq[...] += jnp.sum(misfit * misfit, axis=0, keepdims=True)
            for k, i in enumerate(rows_of(c)):
                new_state[:, i, :] = updated[0:levels, k * cols : (k + 1) * cols]

    def add_to(total, value):
        for half in range(units // 128):
            rows = pl.ds(half * value.shape[0], value.shape[0])
            total[rows, :] += value[:, half * 128 : (half + 1) * 128]

    def back_last(c):
        at = columns(c)
        g = split(lf[:, at] * m[:, at])
        h = h3[:, at]
        add_to(s4, outer_thin(g, split(h)))
        ga[:, at] = times(wdn[...], *g) * (1.0 - h * h)

    def back_third(c):
        at = columns(c)
        g = split(ga[:, at])
        h = h2[:, at]
        add_to(s3, outer(split(h), g))
        gb[:, at] = times(w3n[...], *g) * (1.0 - h * h)

    def back_second(c):
        at = columns(c)
        g = split(gb[:, at])
        h = h1[:, at]
        add_to(s2, outer(split(h), g))
        ga[:, at] = times(w2n[...], *g) * (1.0 - h * h)

    def back_first(c):
        at = columns(c)
        add_to(s1, outer_thin(split(a[:, at]), split(ga[:, at])))

    def adjoint(c):
        at = columns(c)
        adv = m[:, at] + times(w1n[...], *split(ga[:, at]))
        m[:, at] = adv
        x[:, at] = cf[:, at] * adv

    live = []

    def begin(src, acc, recv, out, s, finish):
        live.append(Sum(plan, me, src, acc, recv, out, sems, s, finish))
        live[-1].send()

    def advance(*which):
        for k in which:
            item = live[k]
            if not item.done:
                item.receive()
                if not item.done:
                    item.send()
                else:
                    item.finish()

    factor = 1.0 / math.sqrt(width * n_tx * n_ty)

    def whole(total, rows):
        return jnp.concatenate([total[k * rows : (k + 1) * rows, :] for k in range(units // 128)], axis=1)

    def finish_last():
        up_index = lax.broadcasted_iota(jnp.int32, (deep, levels), 0)
        to_index = lax.broadcasted_iota(jnp.int32, (deep, levels), 1)
        lower = jnp.where((to_index <= up_index) & (up_index < levels), 1.0 / math.sqrt(levels), 0.0)
        raw = whole(sum4, deep).T
        o4[...] = jnp.dot(raw, lower, precision=precise, preferred_element_type=f32) * factor

    def finish_third():
        o3[...] = whole(sum3, units) * factor

    def finish_second():
        o2[...] = whole(sum2, units) * factor

    def finish_first():
        full = whole(sum1, deep)
        o1[...] = full[0:levels] * factor
        loss[0, 0] = jnp.sum(full[levels : levels + 1]) * (0.5 / (width * n_tx * n_ty))

    for copy in column_copies:
        copy.wait()
    turn_columns(0)
    if middle:
        forward(middle)
    for copy in row_copies:
        copy.wait()
    forward(edges)

    for c in edges + middle:
        back_last(c)
    begin(s4, a4, r4, sum4, 3, finish_last)
    for c in edges:
        back_third(c)
    advance(0)
    for c in middle:
        back_third(c)
    begin(s3, a3, r3, sum3, 2, finish_third)
    for c in edges:
        back_second(c)
    advance(1, 0)
    for c in middle:
        back_second(c)
    begin(s2, a2, r2, sum2, 1, finish_second)
    for c in range(count):
        back_first(c)
    for part in range(units // 128):
        squares = jnp.zeros((1, 128), f32)
        if part == 0:
            for k in range(chunk // 128):
                squares = squares + sq[:, k * 128 : (k + 1) * 128]
        s1[part * deep + levels : part * deep + levels + 1, :] = squares
    begin(s1, a1, r1, sum1, 0, finish_first)
    advance(2, 1)
    for c in edges:
        adjoint(c)
    row_copies = exchange_rows(1, x)
    advance(3)
    for c in middle:
        adjoint(c)
    column_copies = exchange_columns(1, x)
    advance(2, 0)

    def finish_rows(rows):
        for i in rows:
            state_grad[:, i, :] = (m[:, row(i)] + laplace(1, x, i))[0:levels]

    for copy in column_copies:
        copy.wait()
    turn_columns(1)
    advance(3, 1)
    finish_rows(range(1, tile_rows - 1))
    advance(2, 3, 0)
    for copy in row_copies:
        copy.wait()
    finish_rows((0, tile_rows - 1))
    while not all(item.done for item in live):
        advance(2, 3, 1, 0)
    for item in live:
        item.drain()


def deliver(*refs):
    *refs, sems = refs
    half = len(refs) // 2
    copies = [pltpu.make_async_copy(refs[k], refs[half + k], sems.at[k]) for k in range(half)]
    for copy in copies:
        copy.start()
    for copy in copies:
        copy.wait()


def body(n_tx, n_ty, state, target, rate, face_map, face_metric, land_mask, w_first, w_second, w_third, w_last):
    levels, tile_rows, tile_cols = state.shape
    units = w_second.shape[0]
    width = tile_rows * tile_cols
    deep = -(-(levels + 1) // 8) * 8
    chunk = min(1024, width)
    unit = 8 * n_tx * n_ty
    f32, bf16 = jnp.float32, jnp.bfloat16

    def padded(rows):
        return -(-rows // unit) * unit

    lanes = units // 128
    small, large = padded(lanes * deep), padded(lanes * units)
    sizes = (small, large, large, small)
    plan = plan_of(n_tx, n_ty)
    steps = 2 * len(plan[0]) + 1
    anywhere = pl.BlockSpec(memory_space=pl.ANY)
    vmem = pl.BlockSpec(memory_space=pltpu.VMEM)
    scratch = (
        [pltpu.VMEM((r, 128), f32) for r in sizes]
        + [pltpu.VMEM((deep, units), f32)]
        + [pltpu.VMEM(w.shape, f32) for w in (state, target, w_first, w_second, w_third, w_last)]
        + [pltpu.VMEM((deep, width), f32)] * 4
        + [pltpu.VMEM((1, width), f32)] * 2
        + [pltpu.VMEM((units, width), f32)] * 5
        + [
            pltpu.VMEM((units, 3 * deep), bf16),
            pltpu.VMEM((units, 3 * units), bf16),
            pltpu.VMEM((units, 3 * units), bf16),
            pltpu.VMEM((deep, 3 * units), bf16),
            pltpu.VMEM((deep, 3 * units), bf16),
            pltpu.VMEM((units, 3 * units), bf16),
            pltpu.VMEM((units, 3 * units), bf16),
            pltpu.VMEM((units, 3 * deep), bf16),
            pltpu.VMEM((1, chunk), f32),
        ]
        + [pltpu.VMEM((r, 128), f32) for r in sizes] * 2
        + [pltpu.VMEM((landing(plan, r), 128), f32) for r in sizes]
        + [
            pltpu.VMEM((2, 2, deep, tile_cols), f32),
            pltpu.VMEM((2, 2, tile_rows, deep), f32),
            pltpu.VMEM((2, 2, tile_rows, deep), f32),
            pltpu.VMEM((2, deep, tile_rows), f32),
            pltpu.SemaphoreType.DMA((6,)),
            pltpu.SemaphoreType.DMA((2, 4, steps, 8)),
            pltpu.SemaphoreType.DMA((2, 2, 4)),
        ]
    )
    outs = (state, state, w_first, w_second, w_third, w_last)
    *results, loss = pl.pallas_call(
        functools.partial(window_kernel, n_tx, n_ty, chunk),
        out_shape=[pltpu.VMEM(o.shape, f32) for o in outs] + [jax.ShapeDtypeStruct((1, 1), f32)],
        in_specs=[anywhere] * 2 + [vmem] * 2 + [pl.BlockSpec(memory_space=pltpu.SMEM), vmem] + [anywhere] * 4,
        out_specs=[vmem] * 6 + [pl.BlockSpec(memory_space=pltpu.SMEM)],
        scratch_shapes=scratch,
        compiler_params=pltpu.CompilerParams(
            collective_id=0, has_side_effects=True, vmem_limit_bytes=57 * 2**20
        ),
        name="window",
    )(state, target, rate, face_map, face_metric, land_mask, w_first, w_second, w_third, w_last)
    results = pl.pallas_call(
        deliver,
        out_shape=[jax.ShapeDtypeStruct(o.shape, f32) for o in outs],
        in_specs=[pl.BlockSpec(memory_space=pl.ANY)] * len(outs),
        out_specs=[pl.BlockSpec(memory_space=pl.ANY)] * len(outs),
        scratch_shapes=[pltpu.SemaphoreType.DMA((len(outs),))],
        compiler_params=pltpu.CompilerParams(vmem_limit_bytes=2**20),
        name="deliver",
    )(*results)
    return (*results, loss.reshape(()))


def solution(mesh):
    tile, flat, copied = P(None, "tx", "ty"), P("tx", "ty"), P()
    return jax.shard_map(
        functools.partial(body, mesh.shape["tx"], mesh.shape["ty"]),
        mesh=mesh,
        in_specs=(tile, tile, flat, flat, copied, flat, copied, copied, copied, copied),
        out_specs=(tile, tile, copied, copied, copied, copied, copied),
        check_vma=False,
    )
```
